32 devices in a mesh: row: 4 (over x, core), col: 8 (over z, y).
Axes of the slice: x: 2, y: 2, z: 4, core: 2. Of those that a mesh axis runs over, the one named last changes fastest.
Arguments:
- features: bfloat16 [8192, 256], P(('col', 'row')), may hold values from -6 to 6
- weight: bfloat16 [256, 256], replicated, may hold values from -0.375 to 0.375
- grad_out: bfloat16 [8192, 256], P(('row', 'col')), may hold values from -6 to 6
- adj_values: bfloat16 [384, 1024, 128], P('row', 'col'), may hold values from -0.15625 to 0.15625
- block_pos: int32 [4, 768], P('row', 'col'), may hold values from 0 to 127, as said below
- block_count: int32 [4, 8], P('row', 'col'), may hold values from 24 to 96, as said below
Outputs:
- activation: bfloat16 [8192, 256], P(('row', 'col'))
- grad_input: bfloat16 [8192, 256], P(('col', 'row'))
- grad_weight: float32 [256, 256], replicated
The draws below stay inside these ranges and needn't reach their ends.
Inputs may be any that keep to these rules, and one draw needn't show every extreme that they name: `block_pos`: within one tile the block positions of all 96 slots are distinct values below 128. `block_count`: some tile has exactly 96 live slots and some tile exactly 24.
All inputs are finite; a program needn't handle non-finite values.
Results may differ from the reference program's by a relative error of at most 0.018.
Values may be sent and summed in bfloat16 or wider, within the bound.
A program may use at most 128 MiB of HBM per device.

```python
import jax
import jax.numpy as jnp
from jax import lax

PB = 2
BS = 128
F = 256
N = 8192
RB = 16
CB = 8
NB_MAX = 96
N_ROW = 4
N_COL = 8


def draw_block_pos(key, part):
    tiles = N_ROW * N_COL
    total = PB * PB * N_ROW * N_COL
    tile_keys = jax.random.split(key, tiles)
    chosen = jax.vmap(lambda single: jax.random.permutation(single, total)[:NB_MAX])(tile_keys)
    return chosen.astype(jnp.int32).reshape(N_ROW, N_COL * NB_MAX)


def draw_block_count(key, part):
    tiles = N_ROW * N_COL
    counts = jax.random.randint(key, (tiles,), NB_MAX // 4, NB_MAX + 1).astype(jnp.int32)
    chosen_tile = jax.random.randint(jax.random.fold_in(key, 7), (), 0, tiles)
    counts = counts.at[chosen_tile].set(NB_MAX)
    other_tile = (chosen_tile + 1) % tiles
    counts = counts.at[other_tile].set(NB_MAX // 4)
    return counts.reshape(N_ROW, N_COL)


def shard_levels(own_key, dims, pieces, least, high):
    factor_of = 1.0
    for position, parts in pieces:
        steps = jax.random.uniform(jax.random.fold_in(jax.random.fold_in(own_key, 6), position), (parts,), jnp.float32, least / len(pieces), high / len(pieces))
        factor_of = factor_of * jnp.repeat(jnp.exp(steps), dims[position] // parts).reshape((-1,) + (1,) * (len(dims) - 1 - position))
    return factor_of


def gaussian(key, dims, scale, limit, cuts=(), kind=jnp.bfloat16):
    level = shard_levels(key, dims, cuts, -0.22, 0.18) if cuts else 1.0
    result = jax.random.normal(key, dims, jnp.float32) * scale * level
    return jnp.minimum(jnp.maximum(result, -limit), limit).astype(kind)


def setup_inputs(seed: int = 0) -> dict:
    splits = jax.random.split(jax.random.key(seed), 7)
    features = gaussian(splits[0], (N, F), 1.0, 6.0, ((0, 32),))
    weight = gaussian(splits[1], (F, F), F ** -0.5, 0.375)
    grad_out = gaussian(splits[2], (N, F), 1.0, 6.0, ((0, 32),))
    adj_values = gaussian(splits[3], (N_ROW * NB_MAX, N_COL * BS, BS), ((10 * NB_MAX * BS // RB) ** -0.5), 0.15625, ((0, 4), (1, 8)))
    block_pos = draw_block_pos(jax.random.fold_in(splits[6], 71), 0)
    block_count = draw_block_count(jax.random.fold_in(splits[6], 71), 0)
    return {"features": features, "weight": weight, "grad_out": grad_out, "adj_values": adj_values, "block_pos": block_pos, "block_count": block_count}


def tile_forward(values, positions, live_count, panel, row_blocks, col_blocks):
    slots = values.shape[0]
    block_size = values.shape[1]
    width = panel.shape[1]
    groups = 6
    per_group = slots // groups
    brow = positions // col_blocks
    bcol = positions % col_blocks
    live = (jnp.arange(slots, dtype=jnp.int32) < live_count).astype(jnp.float32)
    blocks = panel.reshape(col_blocks, block_size, width)

    def step(totals, items):
        vals, rows_idx, cols_idx, alive = items
        picked = blocks[cols_idx].astype(jnp.float32)
        prod = jnp.einsum("kij,kjf->kif", vals.astype(jnp.float32), picked)
        onehot = (rows_idx[None, :] == jnp.arange(row_blocks, dtype=jnp.int32)[:, None]).astype(jnp.float32) * alive[None, :]
        return totals + jnp.einsum("bk,kif->bif", onehot, prod), None

    items = (values.reshape(groups, per_group, block_size, block_size), brow.reshape(groups, per_group), bcol.reshape(groups, per_group), live.reshape(groups, per_group))
    start = jnp.zeros((row_blocks, block_size, width), jnp.float32)
    totals, unused = lax.scan(step, start, items)
    return totals.reshape(row_blocks * block_size, width)


def tile_backward(values, positions, live_count, grads, row_blocks, col_blocks):
    slots = values.shape[0]
    block_size = values.shape[1]
    width = grads.shape[1]
    groups = 6
    per_group = slots // groups
    brow = positions // col_blocks
    bcol = positions % col_blocks
    live = (jnp.arange(slots, dtype=jnp.int32) < live_count).astype(jnp.float32)
    blocks = grads.reshape(row_blocks, block_size, width)

    def step(totals, items):
        vals, rows_idx, cols_idx, alive = items
        picked = blocks[rows_idx].astype(jnp.float32)
        prod = jnp.einsum("kij,kif->kjf", vals.astype(jnp.float32), picked)
        onehot = (cols_idx[None, :] == jnp.arange(col_blocks, dtype=jnp.int32)[:, None]).astype(jnp.float32) * alive[None, :]
        return totals + jnp.einsum("bk,kjf->bjf", onehot, prod), None

    items = (values.reshape(groups, per_group, block_size, block_size), brow.reshape(groups, per_group), bcol.reshape(groups, per_group), live.reshape(groups, per_group))
    start = jnp.zeros((col_blocks, block_size, width), jnp.float32)
    totals, unused = lax.scan(step, start, items)
    return totals.reshape(col_blocks * block_size, width)


def round_part(part):
    rounded = lax.optimization_barrier(part.astype(jnp.bfloat16))
    return rounded.astype(jnp.float32)


def reference(features, weight, grad_out, adj_values, block_pos, block_count):
    rows_tile = RB * BS
    cols_tile = CB * BS
    xw = jnp.dot(features, weight, preferred_element_type=jnp.float32).astype(jnp.bfloat16)
    positions_all = block_pos.reshape(N_ROW, N_COL, NB_MAX)
    value_rows = adj_values.reshape(N_ROW, NB_MAX, N_COL * BS, BS)

    def forward_row(index_row):
        tile_vals = value_rows[index_row]

        def over_cols(totals, index_col):
            vals = lax.dynamic_slice_in_dim(tile_vals, index_col * BS, BS, 1)
            panel = lax.dynamic_slice_in_dim(xw, index_col * cols_tile, cols_tile, 0)
            part = tile_forward(vals, positions_all[index_row, index_col], block_count[index_row, index_col], panel, RB, CB)
            return totals + round_part(part), None

        totals, unused = lax.scan(over_cols, jnp.zeros((rows_tile, F), jnp.float32), jnp.arange(N_COL, dtype=jnp.int32))
        return totals

    hidden = lax.map(forward_row, jnp.arange(N_ROW, dtype=jnp.int32)).reshape(N, F)
    sigma = jax.nn.sigmoid(hidden)
    activation = (hidden * sigma).astype(jnp.bfloat16)
    grad_hidden = (grad_out.astype(jnp.float32) * sigma * (1.0 + hidden * (1.0 - sigma))).astype(jnp.bfloat16)

    def backward_col(index_col):
        def over_rows(totals, index_row):
            vals = lax.dynamic_slice_in_dim(value_rows[index_row], index_col * BS, BS, 1)
            grads = lax.dynamic_slice_in_dim(grad_hidden, index_row * rows_tile, rows_tile, 0)
            part = tile_backward(vals, positions_all[index_row, index_col], block_count[index_row, index_col], grads, RB, CB)
            return totals + round_part(part), None

        totals, unused = lax.scan(over_rows, jnp.zeros((cols_tile, F), jnp.float32), jnp.arange(N_ROW, dtype=jnp.int32))
        return totals

    grad_xw = lax.map(backward_col, jnp.arange(N_COL, dtype=jnp.int32)).reshape(N, F).astype(jnp.bfloat16)
    grad_weight = lax.dot_general(features, grad_xw, (((0,), (0,)), ((), ())), preferred_element_type=jnp.float32)
    grad_input = lax.dot_general(grad_xw, weight, (((1,), (1,)), ((), ())), preferred_element_type=jnp.float32).astype(jnp.bfloat16)
    return activation, grad_input, grad_weight
```

```python
import functools

import jax
import jax.numpy as jnp
from jax import lax
from jax.experimental import pallas as pl
from jax.experimental.pallas import tpu as pltpu
from jax.sharding import PartitionSpec as P

MESH = pl.DeviceIdType.MESH
F32 = jnp.float32
BF16 = jnp.bfloat16
OWN, MATE, NEAR, FAR = 0, 1, 2, 3
END_LAG = 0.5
W_GAPS = (0.3, 3.6, 4.5)


def split_axis(size, inner):
    while size % inner:
        inner -= 1
    return size // inner, inner


def send_order(parts):
    first = [(0, d) for d in (NEAR, FAR, MATE, OWN)]
    far = [(q, d) for q in range(1, parts) for d in (NEAR, FAR)]
    close = [(q, d) for q in range(1, parts) for d in (MATE, OWN)]
    return first + far + close


def plan(parts, order, ci):
    wire, hop, line, extra, work = 2.8 / parts, 1.7, 2.2, 0.8, 0.4
    step = wire + line
    y = {at: 0.4 + wire * (k + 1) + hop for k, at in enumerate(order)}
    events, ready = [], {"rim": [], "cen": []}
    ends = 0.0
    for q in range(parts):
        rim = {d: y[q, d] for d in (NEAR, FAR, MATE)}
        for d in (NEAR, FAR, MATE):
            events.append((rim[d], "rim", "M", q, d))
        events.append((y[q, MATE], "cen", "M", q, MATE))
        join = {d: max(y[q, d], rim[d] + step) for d in (NEAR, FAR)}
        for d in (NEAR, FAR):
            events.append((join[d], "cen", "J", q, d))
        cen = max(y[q, OWN], rim[MATE] + step, join[NEAR] + step) + END_LAG
        out = max(y[q, OWN], y[q, MATE] + step, join[FAR] + step + extra) + END_LAG
        events.append((cen, "cen", "E", q, OWN))
        events.append((out, "rim", "E", q, OWN))
        cen, out = cen + work, out + work
        ends = max(ends, cen, out)
        at_cen = {OWN: cen, NEAR: cen + step, MATE: out + step + wire, FAR: out + step + extra}
        at_rim = {
            OWN: out,
            MATE: cen + step + wire,
            NEAR: at_cen[NEAR] + step,
            FAR: at_cen[FAR] + step,
        }
        for d in (MATE, NEAR, FAR):
            events.append((at_cen[d], "cen", "O", q, d))
            events.append((at_rim[d], "rim", "O", q, d))
        ready["cen"] += [(at_cen[d], q, d) for d in range(4)]
        ready["rim"] += [(at_rim[d], q, d) for d in range(4)]
    there = {}
    for role, pieces in ready.items():
        free = 0.4 + wire * len(order)
        for when, q, d in sorted(pieces):
            free = max(free, when) + wire
            there[d] = max(there.get(d, 0.0), free + hop)
    blocks = []
    for d in range(4):
        here = max(when for role in ready for when, _, at in ready[role] if at == d)
        blocks.append((here + 0.01, d, 0))
        for e in range(1, ci):
            blocks.append((there[d] + 0.01 * e, d, e))
    blocks.sort()
    for when, d, e in blocks[:-1]:
        events.append((when, "all", "B", d, e))
    for k, gap in enumerate(W_GAPS):
        ends += gap
        events.append((ends, "all", "W", k, 0))
    events.append((y[0, NEAR] + 0.02, "all", "P", MATE, 0))
    events.append((y[0, FAR] + 0.02, "all", "P", OWN, 0))
    events.sort(key=lambda event: event[0])
    return events, blocks[-1][1:]


def kernel(
    dims,
    count_ref,
    pos_ref,
    feat_ref,
    weight_ref,
    gout_ref,
    adj_ref,
    act_ref,
    gin_ref,
    gw_ref,
    pos_v,
    inv_v,
    inv_s,
    vals,
    dense,
    dense_t,
    feats,
    pair,
    mine,
    s_in,
    r_in,
    s_out,
    r_out,
    af,
    ghs,
    acc,
    rs_y,
    rr_y,
    rs_z,
    rr_z,
    ws1,
    wr1,
    ws2,
    wr2,
    w4,
    local_sem,
    sem_sent,
    sem_fx,
    sem_fs,
    sem_c,
    sem_a,
    sem_b,
    sem_ry,
    sem_r0,
    sem_rz,
    sem_w,
):
    (nrow, ncol, ro, ri, co, ci, parts) = dims
    slots, bs, _ = adj_ref.shape
    own, width = feat_ref.shape
    piece = own // parts
    row_blocks = dense.shape[0] // bs
    col_blocks = dense.shape[1] // bs
    spots = row_blocks * col_blocks
    row = lax.axis_index("row")
    col = lax.axis_index("col")
    rx, rc = lax.div(row, ri), lax.rem(row, ri)
    cz, cy = lax.div(col, ci), lax.rem(col, ci)

    def remote(src, dst, send, recv, axis, peer):
        return pltpu.make_async_remote_copy(
            src_ref=src,
            dst_ref=dst,
            send_sem=send,
            recv_sem=recv,
            device_id={axis: peer},
            device_id_type=MESH,
        )

    loads = [
        pltpu.make_async_copy(feat_ref, feats.at[row], local_sem.at[0]),
        pltpu.make_async_copy(pos_ref, pos_v, local_sem.at[3]),
        pltpu.make_async_copy(adj_ref, vals.at[pl.ds(0, slots)], local_sem.at[1]),
        pltpu.make_async_copy(weight_ref, pair.at[0], local_sem.at[2]),
        pltpu.make_async_copy(gout_ref, pair.at[1], local_sem.at[2]),
    ]
    for load in loads:
        load.start()

    barrier = pltpu.get_barrier_semaphore()
    for d in range(1, nrow):
        pl.semaphore_signal(
            barrier, inc=1, device_id={"row": lax.rem(row + d, nrow)}, device_id_type=MESH
        )
    for d in range(1, ncol):
        pl.semaphore_signal(
            barrier, inc=1, device_id={"col": lax.rem(col + d, ncol)}, device_id_type=MESH
        )
    vals[slots] = jnp.zeros((bs, bs), vals.dtype)
    loads[1].wait()
    slot = lax.broadcasted_iota(jnp.int32, (spots, slots), 1)
    spot = lax.broadcasted_iota(jnp.int32, (spots, slots), 0)
    hit = (pos_v[...] == spot) & (slot < count_ref[0, 0])
    found = slots + jnp.sum(jnp.where(hit, slot - slots, 0), axis=1, keepdims=True)
    inv_v[...] = jnp.broadcast_to(found, (spots, 128)).T[:8]
    table = pltpu.make_async_copy(inv_v, inv_s, local_sem.at[4])
    table.start()
    loads[0].wait()
    pl.semaphore_wait(barrier, nrow + ncol - 2)

    halves = 2
    half = own // halves

    def feature(block, h, sem, peer):
        at = feats.at[block, pl.ds(h * half, half)]
        return remote(at, at, sem_sent.at[0], sem, "row", peer)

    def feature_x(block, h, d):
        sem = sem_fx.at[(ro - d - 1) * halves + h]
        return feature(block, h, sem, lax.rem(rx + d, ro) * ri + rc)

    def feature_in(block, h):
        for e in range(1, ri):
            feature(block, h, sem_fs.at[0], rx * ri + lax.rem(rc + e, ri)).start()

    for h in range(halves):
        for d in range(1, ro):
            feature_x(row, h, d).start()
    for h in range(halves):
        feature_in(row, h)
    table.wait()
    loads[2].wait()

    def fill(r, carry):
        for c in range(col_blocks):
            tile = vals[inv_s[0, r * col_blocks + c]]
            at = pl.ds(pl.multiple_of(r * bs, bs), bs)
            dense[at, c * bs : (c + 1) * bs] = tile
            dense_t[c * bs : (c + 1) * bs, at] = tile.T
        return carry

    lax.fori_loop(0, row_blocks, fill, 0)
    for h in range(halves):
        for d in range(1, ro):
            block = lax.rem(rx + d, ro) * ri + rc
            feature_x(block, h, ro - d).wait_recv()
            feature_in(block, h)
    if ri > 1:
        at = feats.at[pl.ds(0, ro * (ri - 1))]
        remote(at, at, sem_sent.at[0], sem_fs.at[0], "row", 0).wait_recv()

    def rows(block, size=own):
        return pl.ds(pl.multiple_of(block * size, size), size)

    def forward(block):
        return jnp.dot(
            dense[rows(block), :],
            feats[...].reshape(nrow * own, width),
            preferred_element_type=F32,
        )

    central = lax.rem(lax.div(cz + 1, 2), 2) == 1
    mate = cz + 1 - 2 * lax.rem(cz, 2)
    near = 2 - lax.div(cz, 2)
    place = (cz, mate, near, 3 * (near - 1))

    def cut(q):
        return pl.ds(q * piece, piece)

    def pieces(n, sem):
        at = r_out.at[pl.ds(0, n)]
        remote(at, at, sem_sent.at[0], sem, "col", 0).wait_recv()

    def inner_copy(q, d, e):
        at = d * (ci - 1) + e - 1
        return remote(
            s_in.at[at, cut(q)],
            r_in.at[at, cut(q)],
            sem_sent.at[0],
            sem_c.at[q * 4 + d],
            "col",
            cz * ci + lax.rem(cy + e, ci),
        )

    order = send_order(parts)
    queue = list(order)
    done = set()
    for d in (NEAR, FAR, MATE, OWN):
        for e in range(1, ci):
            s_in[d * (ci - 1) + e - 1] = forward(place[d] * ci + lax.rem(cy + e, ci)).astype(BF16)
        done.add(d)
        while queue and queue[0][1] in done and (queue[0][0] == 0 or len(done) == co):
            for e in range(1, ci):
                inner_copy(*queue[0], e).start()
            queue.pop(0)

    def own_part(d):
        mine[d] = forward(place[d] * ci + cy)

    own_part(NEAR)
    own_part(FAR)
    pltpu.make_async_copy(pair, pair, local_sem.at[2]).wait()

    def joined(q, d, others=()):
        n = ci - 1 + len(others)
        if n:
            pieces(n, sem_c.at[q * 4 + d])
        value = mine[d, cut(q)]
        for e in range(1, ci):
            value = value + r_in[d * (ci - 1) + e - 1, cut(q)].astype(F32)
        for landing in others:
            value = value + r_out[q * 4 + landing].astype(F32)
        return value

    def hop(q, d, landing, peer):
        return remote(
            s_out.at[q * 4 + d],
            r_out.at[q * 4 + landing],
            sem_sent.at[0],
            sem_c.at[q * 4 + (landing if landing > 1 else OWN)],
            "col",
            peer * ci + cy,
        )

    def push(block, q, sem, peer):
        at = ghs.at[block, cut(q)]
        return remote(at, at, sem_sent.at[0], sem, "col", peer)

    def inward(block, q, d):
        for e in range(1, ci):
            sem = sem_b.at[d * (ci - 1) + ci - e - 1]
            push(block, q, sem, cz * ci + lax.rem(cy + e, ci)).start()

    def middle(q, d):
        s_out[q * 4 + d] = joined(q, d).astype(BF16)
        hop(q, d, 0 if d == MATE else d, mate).start()

    def join(q, d):
        s_out[q * 4 + d] = joined(q, d, (d,)).astype(BF16)
        hop(q, d, 1, place[d]).start()

    def end(q, role):
        part = joined(q, OWN, (0, 1)).astype(BF16)
        af[cut(q), :] = part
        hidden = jnp.dot(part, pair[0], preferred_element_type=F32)
        sigma = jax.nn.sigmoid(hidden)
        ghs[col, cut(q)] = (
            pair[1, cut(q)].astype(F32) * sigma * (1.0 + hidden * (1.0 - sigma))
        ).astype(BF16)
        label = NEAR if role == "cen" else FAR
        push(col, q, sem_a.at[q * 3 + label - 1], near * ci + cy).start()
        push(col, q, sem_a.at[q * 3 + MATE - 1], mate * ci + cy).start()
        inward(col, q, OWN)
        act_ref[cut(q), :] = (hidden * sigma).astype(BF16)

    def outer(q, d, role):
        block = place[d] * ci + cy
        push(block, q, sem_a.at[q * 3 + d - 1], 0).wait_recv()
        if role == "cen" and d > 1:
            push(block, q, sem_a.at[q * 3 + d - 1], mate * ci + cy).start()
        inward(block, q, d)

    seen = []

    def gathered(d, e):
        block = place[d] * ci + lax.rem(cy + e, ci)
        if e:
            at = ghs.at[block]
            remote(at, at, sem_sent.at[0], sem_b.at[d * (ci - 1) + e - 1], "col", 0).wait_recv()
        return block

    def backward(d, e):
        block = gathered(d, e)
        term = jnp.dot(dense_t[:, rows(block)], ghs[block], preferred_element_type=F32)
        acc[...] = acc[...] + term if seen else term
        seen.append(1)

    rows1 = width // nrow
    rows2 = rows1 // ncol

    def w_send(k, source, target, axis, peer):
        remote(source, target, sem_w.at[0, k], sem_w.at[1, k], axis, peer).start()

    w_refs = (wr1, wr2, w4.at[0, pl.ds(0, nrow - 1)], w4.at[pl.ds(0, ncol - 1)])

    def w_copy(k):
        return remote(w_refs[k], w_refs[k], sem_w.at[0, k], sem_w.at[1, k], "col", 0)

    def weight_step(k):
        if k == 0:
            grad = jnp.dot(af[...].T, ghs[col], preferred_element_type=F32)
            ws1[...] = grad.astype(BF16).reshape(nrow, rows1, width)
            for d in range(1, nrow):
                peer = lax.rem(row + d, nrow)
                w_send(0, ws1.at[peer], wr1.at[d - 1], "row", peer)
        elif k == 1:
            w_copy(0).wait_recv()
            share = ws1[row].astype(F32)
            for d in range(1, nrow):
                share = share + wr1[d - 1].astype(F32)
            for j in range(ncol):
                ws2[j] = share[j * rows2 : (j + 1) * rows2].astype(BF16)
            for d in range(1, ncol):
                peer = lax.rem(col + d, ncol)
                w_send(1, ws2.at[peer], wr2.at[d - 1], "col", peer)
        elif k == 2:
            w_copy(1).wait_recv()
            share = ws2[col].astype(F32)
            for d in range(1, ncol):
                share = share + wr2[d - 1].astype(F32)
            w4[col, row] = share.astype(BF16)
            for d in range(1, nrow):
                at = w4.at[col, row]
                w_send(2, at, at, "row", lax.rem(row + d, nrow))
        elif k == 3:
            w_copy(2).wait_recv()
            for d in range(1, ncol):
                w_send(3, w4.at[col], w4.at[col], "col", lax.rem(col + d, ncol))
        else:
            w_copy(3).wait_recv()
            for r in range(nrow):
                for k in range(ncol):
                    at = r * rows1 + k * rows2
                    gw_ref[at : at + rows2, :] = w4[k, r].astype(F32)

    def act_on(event, role):
        _, _, kind, a, b = event
        if kind == "M":
            middle(a, b)
        elif kind == "J":
            join(a, b)
        elif kind == "E":
            end(a, role)
        elif kind == "O":
            outer(a, b, role)
        elif kind == "B":
            backward(a, b)
        elif kind == "P":
            own_part(a)
        else:
            weight_step(a)

    events, final = plan(parts, order, ci)
    pending = {"rim": [], "cen": []}

    def flush():
        for role, here in (("cen", central), ("rim", jnp.logical_not(central))):
            todo = pending[role]
            pending[role] = []
            if todo:

                @pl.when(here)
                def _():
                    for event in todo:
                        act_on(event, role)

    for event in events:
        if event[1] == "all":
            flush()
            act_on(event, "all")
        else:
            pending[event[1]].append(event)
    flush()

    block = gathered(*final)
    last = ghs[block]

    def finished(to, core):
        at = rows(to * ri + core)
        return acc[at, :] + jnp.dot(
            dense_t[at, rows(block)], last, preferred_element_type=F32
        )

    def sibling(d, e, p):
        at = d * (ri - 1) + e - 1
        return remote(
            rs_y.at[at, cut(p)],
            rr_y.at[at, cut(p)],
            sem_sent.at[0],
            sem_ry.at[(d - 1) * parts + p] if d else sem_r0.at[0],
            "row",
            rx * ri + lax.rem(rc + e, ri),
        )

    def across(d, p):
        return remote(
            rs_z.at[d - 1, cut(p)],
            rr_z.at[d - 1, cut(p)],
            sem_sent.at[0],
            sem_rz.at[(d - 1) * parts + p],
            "row",
            lax.rem(rx + d, ro) * ri + rc,
        )

    targets = list(range(1, ro)) + [0]
    for d in targets:
        to = lax.rem(rx + d, ro)
        for e in range(1, ri):
            rs_y[d * (ri - 1) + e - 1] = finished(to, lax.rem(rc + e, ri)).astype(BF16)
            for p in range(parts):
                sibling(d, e, p).start()
    for d in targets:
        at = rows(lax.rem(rx + d, ro) * ri + rc)
        acc[at, :] = finished(lax.rem(rx + d, ro), rc)

    def chip_sum(d, p):
        at = pl.ds(pl.multiple_of((lax.rem(rx + d, ro) * ri + rc) * own + p * piece, piece), piece)
        value = acc[at, :]
        for e in range(1, ri):
            value = value + rr_y[d * (ri - 1) + e - 1, cut(p)].astype(F32)
        return value

    for p in range(parts):
        for d in range(1, ro):
            if ri > 1:
                pieces(ri - 1, sem_ry.at[(d - 1) * parts + p])
            rs_z[d - 1, cut(p)] = chip_sum(d, p).astype(BF16)
            across(d, p).start()
    weight_step(3)
    if ri > 1:
        at = rr_y.at[pl.ds(0, ri - 1)]
        remote(at, at, sem_sent.at[0], sem_r0.at[0], "row", 0).wait_recv()
    for p in range(parts):
        value = chip_sum(0, p)
        for d in range(1, ro):
            across(d, p).wait_recv()
            value = value + rr_z[d - 1, cut(p)].astype(F32)
        gin_ref[cut(p), :] = lax.dot_general(
            value.astype(BF16), pair[0], (((1,), (1,)), ((), ())), preferred_element_type=F32
        ).astype(BF16)
    weight_step(4)

    def all_sent(extra):
        blocks = (ro - 1) + ro * (ri - 1)
        blocks += co * (ci - 1) + (co - 1) + 2 + co * (ci - 1) + extra
        blocks += ro * (ri - 1) + (ro - 1)
        at = dense.at[pl.ds(0, blocks * own * width // dense.shape[1])]
        remote(at, at, sem_sent.at[0], sem_sent.at[0], "row", 0).wait_send()

    @pl.when(central)
    def _():
        all_sent(2)

    @pl.when(jnp.logical_not(central))
    def _():
        all_sent(0)

    for k in range(4):
        w_copy(k).wait_send()


def hand_on(a_in, b_in, c_in, a_out, b_out, c_out, sems):
    copies = [
        pltpu.make_async_copy(source, target, sems.at[k])
        for k, (source, target) in enumerate(((a_in, a_out), (b_in, b_out), (c_in, c_out)))
    ]
    for copy in copies:
        copy.start()
    for copy in copies:
        copy.wait()


def solution(mesh):
    nrow, ncol = mesh.shape["row"], mesh.shape["col"]
    ro, ri = split_axis(nrow, 2)
    co = 4
    ci = ncol // co
    parts = 4
    dims = (nrow, ncol, ro, ri, co, ci, parts)

    def body(features, weight, grad_out, adj_values, block_pos, block_count):
        own, width = features.shape
        slots, bs, _ = adj_values.shape
        rows_tile = own * ncol
        cols_tile = own * nrow
        spots = (rows_tile // bs) * (cols_tile // bs)
        piece = own // parts
        rows1 = width // nrow
        rows2 = rows1 // ncol
        dma = pltpu.SemaphoreType.DMA

        def block(n, rows, dtype=BF16):
            return pltpu.VMEM((max(n, 1), rows, width), dtype)

        scratch = [
            pltpu.VMEM((1, slots), jnp.int32),
            pltpu.VMEM((8, spots), jnp.int32),
            pltpu.SMEM((8, spots), jnp.int32),
            pltpu.VMEM((slots + 1, bs, bs), BF16),
            pltpu.VMEM((rows_tile, cols_tile), BF16),
            pltpu.VMEM((cols_tile, rows_tile), BF16),
            block(nrow, own),
            block(2, own),
            block(co, own, F32),
            block(co * (ci - 1), own),
            block(co * (ci - 1), own),
            block(parts * 4, piece),
            block(parts * 4, piece),
            pltpu.VMEM((own, width), BF16),
            block(ncol, own),
            pltpu.VMEM((cols_tile, width), F32),
            block(ro * (ri - 1), own),
            block(ro * (ri - 1), own),
            block(ro - 1, own),
            block(ro - 1, own),
            block(nrow, rows1),
            block(nrow - 1, rows1),
            block(ncol, rows2),
            block(ncol - 1, rows2),
            pltpu.VMEM((ncol, nrow, rows2, width), BF16),
            dma((5,)),
            dma((1,)),
            dma((max(2 * (ro - 1), 1),)),
            dma((1,)),
            dma((parts * 4,)),
            dma((parts * 3,)),
            dma((max(co * (ci - 1), 1),)),
            dma((max(parts * (ro - 1), 1),)),
            dma((1,)),
            dma((max(parts * (ro - 1), 1),)),
            dma((2, 4)),
        ]
        vmem = pl.BlockSpec(memory_space=pltpu.VMEM)
        anyspace = pl.BlockSpec(memory_space=pl.ANY)
        shapes = (
            jax.ShapeDtypeStruct((own, width), BF16),
            jax.ShapeDtypeStruct((own, width), BF16),
            jax.ShapeDtypeStruct((width, width), F32),
        )
        held = sum(
            2 * ref.dtype.itemsize * functools.reduce(lambda a, b: a * b, ref.shape, 1) // 2
            for ref in scratch
            if getattr(ref, "memory_space", None) == pltpu.VMEM
        )
        outs = pl.pallas_call(
            functools.partial(kernel, dims),
            out_shape=shapes,
            in_specs=[pl.BlockSpec(memory_space=pltpu.SMEM)] + [anyspace] * 5,
            out_specs=[vmem] * 3,
            scratch_shapes=scratch,
            compiler_params=pltpu.CompilerParams(
                collective_id=0,
                has_side_effects=True,
                vmem_limit_bytes=min(held + (6 << 20), 66 * 1000 * 1000),
            ),
        )(
            block_count,
            *(
                pltpu.with_memory_space_constraint(x, pltpu.HBM)
                for x in (block_pos, features, weight, grad_out, adj_values)
            ),
        )
        return pl.pallas_call(
            hand_on,
            out_shape=shapes,
            in_specs=[anyspace] * 3,
            out_specs=[anyspace] * 3,
            scratch_shapes=[dma((3,))],
            compiler_params=pltpu.CompilerParams(vmem_limit_bytes=1 << 20),
        )(*outs)

    placed = (
        P(("col", "row"), None),
        P(),
        P(("row", "col"), None),
        P("row", "col", None),
        P("row", "col"),
        P("row", "col"),
    )
    return jax.shard_map(
        body,
        mesh=mesh,
        in_specs=placed,
        out_specs=(P(("row", "col"), None), P(("col", "row"), None), P()),
        check_vma=False,
    )
```

```python
import functools

import jax
import jax.numpy as jnp
from jax import lax
from jax.experimental import pallas as pl
from jax.experimental.pallas import tpu as pltpu
from jax.sharding import PartitionSpec as P

MESH = pl.DeviceIdType.MESH
F32 = jnp.float32
BF16 = jnp.bfloat16
OWN, MATE, NEAR, FAR = 0, 1, 2, 3
PARTS = 4
ORDER = (
    (0, 2), (0, 3), (2, 3), (1, 3), (1, 2), (0, 1), (3, 3), (3, 2),
    (2, 2), (3, 1), (1, 1), (2, 1), (0, 0), (1, 0), (2, 0), (3, 0),
)
RIM = (
    ("P", 2, 0), ("P", 3, 0), ("P", 1, 0), ("M", 0, 2), ("P", 0, 0), ("M", 0, 3),
    ("M", 2, 3), ("M", 1, 3), ("M", 1, 2), ("M", 0, 1), ("M", 3, 3), ("M", 3, 2),
    ("M", 2, 2), ("M", 3, 1), ("M", 1, 1), ("M", 2, 1), ("E", 0, 0), ("E", 1, 0),
    ("E", 2, 0), ("E", 3, 0), ("W", 0, 0), ("B", 0, 0), ("O", 0, 1), ("O", 1, 1),
    ("O", 3, 1), ("O", 0, 2), ("W", 1, 0), ("O", 2, 1), ("B", 1, 0), ("O", 0, 3),
    ("O", 1, 2), ("O", 3, 2), ("O", 1, 3), ("O", 2, 2), ("B", 2, 0), ("O", 2, 3),
    ("O", 3, 3), ("B", 3, 0), ("B", 0, 1), ("B", 1, 1), ("W", 2, 0), ("B", 2, 1),
    ("B", 3, 1),
)
CENTRAL = (
    ("P", 2, 0), ("P", 3, 0), ("P", 1, 0), ("P", 0, 0), ("J", 0, 2), ("M", 0, 1),
    ("J", 0, 3), ("J", 2, 3), ("J", 1, 3), ("J", 1, 2), ("M", 3, 1), ("M", 1, 1),
    ("J", 3, 3), ("M", 2, 1), ("J", 3, 2), ("E", 0, 0), ("J", 2, 2), ("E", 1, 0),
    ("E", 3, 0), ("O", 0, 2), ("O", 0, 1), ("E", 2, 0), ("W", 0, 0), ("B", 0, 0),
    ("O", 0, 3), ("O", 1, 2), ("O", 1, 1), ("O", 3, 2), ("O", 1, 3), ("O", 2, 1),
    ("O", 2, 2), ("W", 1, 0), ("B", 2, 0), ("O", 2, 3), ("O", 3, 1), ("B", 1, 0),
    ("O", 3, 3), ("B", 3, 0), ("B", 0, 1), ("B", 2, 1), ("W", 2, 0), ("B", 1, 1),
    ("B", 3, 1),
)


def split_axis(size, inner):
    while size % inner:
        inner -= 1
    return size // inner, inner


def kernel(
    dims,
    count_ref,
    pos_ref,
    feat_ref,
    weight_ref,
    gout_ref,
    adj_ref,
    act_ref,
    gin_ref,
    gw_ref,
    pos_v,
    inv_v,
    inv_s,
    vals,
    dense,
    dense_t,
    feats,
    pair,
    mine,
    s_in,
    r_in,
    s_out,
    r_out,
    af,
    ghs,
    acc,
    rs_y,
    rr_y,
    rs_z,
    rr_z,
    ws1,
    wr1,
    ws2,
    wr2,
    w4,
    local_sem,
    sem_up,
    sem_sent,
    sem_fx,
    sem_fs,
    sem_c,
    sem_a,
    sem_b,
    sem_ry,
    sem_r0,
    sem_rz,
    sem_w,
):
    (nrow, ncol, ro, ri, co, ci, parts) = dims
    slots, bs, _ = adj_ref.shape
    own, width = feat_ref.shape
    piece = own // parts
    row_blocks = dense.shape[0] // bs
    col_blocks = dense.shape[1] // bs
    spots = row_blocks * col_blocks
    row = lax.axis_index("row")
    col = lax.axis_index("col")
    rx, rc = lax.div(row, ri), lax.rem(row, ri)
    cz, cy = lax.div(col, ci), lax.rem(col, ci)

    def remote(src, dst, send, recv, axis, peer):
        return pltpu.make_async_remote_copy(
            src_ref=src,
            dst_ref=dst,
            send_sem=send,
            recv_sem=recv,
            device_id={axis: peer},
            device_id_type=MESH,
        )

    loads = [
        pltpu.make_async_copy(feat_ref, feats.at[row], local_sem.at[0]),
        pltpu.make_async_copy(pos_ref, pos_v, local_sem.at[3]),
        pltpu.make_async_copy(adj_ref, vals.at[pl.ds(0, slots)], local_sem.at[1]),
        pltpu.make_async_copy(weight_ref, pair.at[0], local_sem.at[2]),
        pltpu.make_async_copy(gout_ref, pair.at[1], local_sem.at[2]),
    ]
    for load in loads[:2]:
        load.start()

    barrier = pltpu.get_barrier_semaphore()
    for d in range(1, nrow):
        pl.semaphore_signal(
            barrier, inc=1, device_id={"row": lax.rem(row + d, nrow)}, device_id_type=MESH
        )
    for e in range(1, ci):
        pl.semaphore_signal(
            barrier, inc=1, device_id={"col": cz * ci + lax.rem(cy + e, ci)}, device_id_type=MESH
        )

    def greet(sem, d):
        at = cz + d

        @pl.when((at >= 0) & (at < co))
        def _():
            for e in range(ci):
                pl.semaphore_signal(
                    sem, inc=1, device_id={"col": at * ci + e}, device_id_type=MESH
                )

    for d in range(1, co):
        greet(barrier, d)
    vals[slots] = jnp.zeros((bs, bs), vals.dtype)
    loads[1].wait()
    slot = lax.broadcasted_iota(jnp.int32, (spots, slots), 1)
    spot = lax.broadcasted_iota(jnp.int32, (spots, slots), 0)
    hit = (pos_v[...] == spot) & (slot < count_ref[0, 0])
    found = slots + jnp.sum(jnp.where(hit, slot - slots, 0), axis=1, keepdims=True)
    inv_v[...] = jnp.broadcast_to(found, (spots, 128)).T[:8]
    table = pltpu.make_async_copy(inv_v, inv_s, local_sem.at[4])
    table.start()
    loads[0].wait()
    for load in loads[2:]:
        load.start()
    pl.semaphore_wait(barrier, nrow - 1 + ci - 1 + cz * ci)
    for d in range(1, co):
        greet(sem_up, -d)

    halves = 2
    half = own // halves

    def feature(block, h, sem, peer):
        at = feats.at[block, pl.ds(h * half, half)]
        return remote(at, at, sem_sent.at[0], sem, "row", peer)

    def feature_x(block, h, d):
        sem = sem_fx.at[(ro - d - 1) * halves + h]
        return feature(block, h, sem, lax.rem(rx + d, ro) * ri + rc)

    def feature_in(block, h):
        for e in range(1, ri):
            feature(block, h, sem_fs.at[0], rx * ri + lax.rem(rc + e, ri)).start()

    for h in range(halves):
        for d in range(1, ro):
            feature_x(row, h, d).start()
    for h in range(halves):
        feature_in(row, h)
    table.wait()
    loads[2].wait()

    def fill(r, carry):
        for c in range(col_blocks):
            tile = vals[inv_s[0, r * col_blocks + c]]
            at = pl.ds(pl.multiple_of(r * bs, bs), bs)
            dense[at, c * bs : (c + 1) * bs] = tile
            dense_t[c * bs : (c + 1) * bs, at] = tile.T
        return carry

    lax.fori_loop(0, row_blocks, fill, 0)
    for h in range(halves):
        for d in range(1, ro):
            block = lax.rem(rx + d, ro) * ri + rc
            feature_x(block, h, ro - d).wait_recv()
            feature_in(block, h)
    if ri > 1:
        at = feats.at[pl.ds(0, ro * (ri - 1))]
        remote(at, at, sem_sent.at[0], sem_fs.at[0], "row", 0).wait_recv()

    def rows(block, size=own):
        return pl.ds(pl.multiple_of(block * size, size), size)

    def forward(block):
        return jnp.dot(
            dense[rows(block), :],
            feats[...].reshape(nrow * own, width),
            preferred_element_type=F32,
        )

    central = lax.rem(lax.div(cz + 1, 2), 2) == 1
    mate = cz + 1 - 2 * lax.rem(cz, 2)
    near = 2 - lax.div(cz, 2)
    place = (cz, mate, near, 3 * (near - 1))

    def cut(q):
        return pl.ds(q * piece, piece)

    def pieces(n, sem):
        at = r_out.at[pl.ds(0, n)]
        remote(at, at, sem_sent.at[0], sem, "col", 0).wait_recv()

    def inner_copy(q, d, e):
        at = d * (ci - 1) + e - 1
        return remote(
            s_in.at[at, cut(q)],
            r_in.at[at, cut(q)],
            sem_sent.at[0],
            sem_c.at[q * 4 + d],
            "col",
            cz * ci + lax.rem(cy + e, ci),
        )

    def partial(targets, queue):
        done = []
        queue = list(queue)
        for d in targets:
            for e in range(1, ci):
                block = place[d] * ci + lax.rem(cy + e, ci)
                s_in[d * (ci - 1) + e - 1] = forward(block).astype(BF16)
            done.append(d)
            while queue and (queue[0][1] in done or d == targets[-1]):
                for e in range(1, ci):
                    inner_copy(*queue[0], e).start()
                queue.pop(0)

    partial((NEAR, FAR, MATE, OWN), ORDER)

    def own_part(d):
        mine[d] = forward(place[d] * ci + cy)

    pltpu.make_async_copy(pair, pair, local_sem.at[2]).wait()

    def joined(q, d, others=()):
        n = ci - 1 + len(others)
        if n:
            pieces(n, sem_c.at[q * 4 + d])
        value = mine[d, cut(q)]
        for e in range(1, ci):
            value = value + r_in[d * (ci - 1) + e - 1, cut(q)].astype(F32)
        for landing in others:
            value = value + r_out[q * 4 + landing].astype(F32)
        return value

    def hop(q, d, landing, peer):
        return remote(
            s_out.at[q * 4 + d],
            r_out.at[q * 4 + landing],
            sem_sent.at[0],
            sem_c.at[q * 4 + (landing if landing > 1 else OWN)],
            "col",
            peer * ci + cy,
        )

    def push(block, q, sem, peer):
        at = ghs.at[block, cut(q)]
        return remote(at, at, sem_sent.at[0], sem, "col", peer)

    def inward(block, q, d):
        for e in range(1, ci):
            sem = sem_b.at[d * (ci - 1) + ci - e - 1]
            push(block, q, sem, cz * ci + lax.rem(cy + e, ci)).start()

    def middle(q, d):
        s_out[q * 4 + d] = joined(q, d).astype(BF16)
        hop(q, d, 0 if d == MATE else d, mate).start()

    def join(q, d):
        s_out[q * 4 + d] = joined(q, d, (d,)).astype(BF16)
        hop(q, d, 1, place[d]).start()

    def end(q, role):
        part = joined(q, OWN, (0, 1)).astype(BF16)
        af[cut(q), :] = part
        hidden = jnp.dot(part, pair[0], preferred_element_type=F32)
        sigma = jax.nn.sigmoid(hidden)
        ghs[col, cut(q)] = (
            pair[1, cut(q)].astype(F32) * sigma * (1.0 + hidden * (1.0 - sigma))
        ).astype(BF16)
        label = NEAR if role == "cen" else FAR
        push(col, q, sem_a.at[q * 3 + label - 1], near * ci + cy).start()
        push(col, q, sem_a.at[q * 3 + MATE - 1], mate * ci + cy).start()
        inward(col, q, OWN)
        act_ref[cut(q), :] = (hidden * sigma).astype(BF16)

    def outer(q, d, role):
        block = place[d] * ci + cy
        push(block, q, sem_a.at[q * 3 + d - 1], 0).wait_recv()
        if role == "cen" and d > 1:
            push(block, q, sem_a.at[q * 3 + d - 1], mate * ci + cy).start()
        inward(block, q, d)

    final = FAR, ci - 1

    def gathered(d, e):
        block = place[d] * ci + lax.rem(cy + e, ci)
        if e:
            at = ghs.at[block]
            remote(at, at, sem_sent.at[0], sem_b.at[d * (ci - 1) + e - 1], "col", 0).wait_recv()
        return block

    def backward(d, others, seen):
        for e in range(1, ci) if others else (0,):
            if (d, e) == final:
                continue
            block = gathered(d, e)
            term = jnp.dot(dense_t[:, rows(block)], ghs[block], preferred_element_type=F32)
            acc[...] = acc[...] + term if seen else term
            seen.append(1)

    rows1 = width // nrow
    rows2 = rows1 // ncol

    def w_send(k, source, target, axis, peer):
        remote(source, target, sem_w.at[0, k], sem_w.at[1, k], axis, peer).start()

    w_refs = (wr1, wr2, w4.at[0, pl.ds(0, nrow - 1)], w4.at[pl.ds(0, ncol - 1)])

    def w_copy(k):
        return remote(w_refs[k], w_refs[k], sem_w.at[0, k], sem_w.at[1, k], "col", 0)

    def weight_step(k):
        if k == 0:
            grad = jnp.dot(af[...].T, ghs[col], preferred_element_type=F32)
            ws1[...] = grad.astype(BF16).reshape(nrow, rows1, width)
            for d in range(1, nrow):
                peer = lax.rem(row + d, nrow)
                w_send(0, ws1.at[peer], wr1.at[d - 1], "row", peer)
        elif k == 1:
            w_copy(0).wait_recv()
            share = ws1[row].astype(F32)
            for d in range(1, nrow):
                share = share + wr1[d - 1].astype(F32)
            for j in range(ncol):
                ws2[j] = share[j * rows2 : (j + 1) * rows2].astype(BF16)
            for d in range(1, ncol):
                peer = lax.rem(col + d, ncol)
                w_send(1, ws2.at[peer], wr2.at[d - 1], "col", peer)
        elif k == 2:
            w_copy(1).wait_recv()
            share = ws2[col].astype(F32)
            for d in range(1, ncol):
                share = share + wr2[d - 1].astype(F32)
            w4[col, row] = share.astype(BF16)
            for d in range(1, nrow):
                at = w4.at[col, row]
                w_send(2, at, at, "row", lax.rem(row + d, nrow))
        elif k == 3:
            w_copy(2).wait_recv()
            for d in range(1, ncol):
                w_send(3, w4.at[col], w4.at[col], "col", lax.rem(col + d, ncol))
        else:
            w_copy(3).wait_recv()
            for r in range(nrow):
                for k in range(ncol):
                    at = r * rows1 + k * rows2
                    gw_ref[at : at + rows2, :] = w4[k, r].astype(F32)

    def act_on(event, role, seen):
        kind, a, b = event
        if kind == "M":
            middle(a, b)
        elif kind == "J":
            join(a, b)
        elif kind == "E":
            end(a, role)
        elif kind == "O":
            outer(a, b, role)
        elif kind == "B":
            backward(a, b, seen)
        elif kind == "P":
            own_part(a)
        else:
            weight_step(a)

    @pl.when(cz < co - 1)
    def _():
        pl.semaphore_wait(sem_up, (co - 1 - cz) * ci)


    @pl.when(central)
    def _():
        seen = []
        for event in CENTRAL:
            act_on(event, "cen", seen)

    @pl.when(jnp.logical_not(central))
    def _():
        seen = []
        for event in RIM:
            act_on(event, "rim", seen)

    block = gathered(*final)
    last = ghs[block]

    def finished(to, core):
        at = rows(to * ri + core)
        return acc[at, :] + jnp.dot(
            dense_t[at, rows(block)], last, preferred_element_type=F32
        )

    def sibling(d, e, p):
        at = d * (ri - 1) + e - 1
        return remote(
            rs_y.at[at, cut(p)],
            rr_y.at[at, cut(p)],
            sem_sent.at[0],
            sem_ry.at[(d - 1) * parts + p] if d else sem_r0.at[0],
            "row",
            rx * ri + lax.rem(rc + e, ri),
        )

    def across(d, p):
        return remote(
            rs_z.at[d - 1, cut(p)],
            rr_z.at[d - 1, cut(p)],
            sem_sent.at[0],
            sem_rz.at[(d - 1) * parts + p],
            "row",
            lax.rem(rx + d, ro) * ri + rc,
        )

    def to_siblings(d):
        to = lax.rem(rx + d, ro)
        for e in range(1, ri):
            rs_y[d * (ri - 1) + e - 1] = finished(to, lax.rem(rc + e, ri)).astype(BF16)
            for p in range(parts):
                sibling(d, e, p).start()

    def kept(d):
        at = rows(lax.rem(rx + d, ro) * ri + rc)
        acc[at, :] = finished(lax.rem(rx + d, ro), rc)

    for d in range(1, ro):
        to_siblings(d)
    for d in range(1, ro):
        kept(d)
    to_siblings(0)

    def chip_sum(d, p):
        at = pl.ds(pl.multiple_of((lax.rem(rx + d, ro) * ri + rc) * own + p * piece, piece), piece)
        value = acc[at, :]
        for e in range(1, ri):
            value = value + rr_y[d * (ri - 1) + e - 1, cut(p)].astype(F32)
        return value

    for p in range(parts):
        for d in range(1, ro):
            if ri > 1:
                pieces(ri - 1, sem_ry.at[(d - 1) * parts + p])
            rs_z[d - 1, cut(p)] = chip_sum(d, p).astype(BF16)
            across(d, p).start()
    kept(0)
    weight_step(3)
    if ri > 1:
        at = rr_y.at[pl.ds(0, ri - 1)]
        remote(at, at, sem_sent.at[0], sem_r0.at[0], "row", 0).wait_recv()
    for p in range(parts):
        value = chip_sum(0, p)
        for d in range(1, ro):
            across(d, p).wait_recv()
            value = value + rr_z[d - 1, cut(p)].astype(F32)
        gin_ref[cut(p), :] = lax.dot_general(
            value.astype(BF16), pair[0], (((1,), (1,)), ((), ())), preferred_element_type=F32
        ).astype(BF16)
    weight_step(4)

    def all_sent(extra):
        blocks = (ro - 1) + ro * (ri - 1)
        blocks += co * (ci - 1) + (co - 1) + 2 + co * (ci - 1) + extra
        blocks += ro * (ri - 1) + (ro - 1)
        at = dense.at[pl.ds(0, blocks * own * width // dense.shape[1])]
        remote(at, at, sem_sent.at[0], sem_sent.at[0], "row", 0).wait_send()

    @pl.when(central)
    def _():
        all_sent(2)

    @pl.when(jnp.logical_not(central))
    def _():
        all_sent(0)

    for k in range(4):
        w_copy(k).wait_send()


def hand_on(a_in, b_in, c_in, a_out, b_out, c_out, sems):
    copies = [
        pltpu.make_async_copy(source, target, sems.at[k])
        for k, (source, target) in enumerate(((a_in, a_out), (b_in, b_out), (c_in, c_out)))
    ]
    for copy in copies:
        copy.start()
    for copy in copies:
        copy.wait()


def solution(mesh):
    nrow, ncol = mesh.shape["row"], mesh.shape["col"]
    ro, ri = split_axis(nrow, 2)
    co = 4
    ci = ncol // co
    parts = PARTS
    dims = (nrow, ncol, ro, ri, co, ci, parts)

    def body(features, weight, grad_out, adj_values, block_pos, block_count):
        own, width = features.shape
        slots, bs, _ = adj_values.shape
        rows_tile = own * ncol
        cols_tile = own * nrow
        spots = (rows_tile // bs) * (cols_tile // bs)
        piece = own // parts
        rows1 = width // nrow
        rows2 = rows1 // ncol
        dma = pltpu.SemaphoreType.DMA

        def block(n, rows, dtype=BF16):
            return pltpu.VMEM((max(n, 1), rows, width), dtype)

        scratch = [
            pltpu.VMEM((1, slots), jnp.int32),
            pltpu.VMEM((8, spots), jnp.int32),
            pltpu.SMEM((8, spots), jnp.int32),
            pltpu.VMEM((slots + 1, bs, bs), BF16),
            pltpu.VMEM((rows_tile, cols_tile), BF16),
            pltpu.VMEM((cols_tile, rows_tile), BF16),
            block(nrow, own),
            block(2, own),
            block(co, own, F32),
            block(co * (ci - 1), own),
            block(co * (ci - 1), own),
            block(parts * 4, piece),
            block(parts * 4, piece),
            pltpu.VMEM((own, width), BF16),
            block(ncol, own),
            pltpu.VMEM((cols_tile, width), F32),
            block(ro * (ri - 1), own),
            block(ro * (ri - 1), own),
            block(ro - 1, own),
            block(ro - 1, own),
            block(nrow, rows1),
            block(nrow - 1, rows1),
            block(ncol, rows2),
            block(ncol - 1, rows2),
            pltpu.VMEM((ncol, nrow, rows2, width), BF16),
            dma((5,)),
            pltpu.SemaphoreType.REGULAR,
            dma((1,)),
            dma((max(2 * (ro - 1), 1),)),
            dma((1,)),
            dma((parts * 4,)),
            dma((parts * 3,)),
            dma((max(co * (ci - 1), 1),)),
            dma((max(parts * (ro - 1), 1),)),
            dma((1,)),
            dma((max(parts * (ro - 1), 1),)),
            dma((2, 4)),
        ]
        vmem = pl.BlockSpec(memory_space=pltpu.VMEM)
        anyspace = pl.BlockSpec(memory_space=pl.ANY)
        shapes = (
            jax.ShapeDtypeStruct((own, width), BF16),
            jax.ShapeDtypeStruct((own, width), BF16),
            jax.ShapeDtypeStruct((width, width), F32),
        )
        held = sum(
            2 * ref.dtype.itemsize * functools.reduce(lambda a, b: a * b, ref.shape, 1) // 2
            for ref in scratch
            if getattr(ref, "memory_space", None) == pltpu.VMEM
        )
        outs = pl.pallas_call(
            functools.partial(kernel, dims),
            out_shape=shapes,
            in_specs=[pl.BlockSpec(memory_space=pltpu.SMEM)] + [anyspace] * 5,
            out_specs=[vmem] * 3,
            scratch_shapes=scratch,
            compiler_params=pltpu.CompilerParams(
                collective_id=0,
                has_side_effects=True,
                vmem_limit_bytes=min(held + (6 << 20), 66 * 1000 * 1000),
            ),
        )(
            block_count,
            *(
                pltpu.with_memory_space_constraint(x, pltpu.HBM)
                for x in (block_pos, features, weight, grad_out, adj_values)
            ),
        )
        return pl.pallas_call(
            hand_on,
            out_shape=shapes,
            in_specs=[anyspace] * 3,
            out_specs=[anyspace] * 3,
            scratch_shapes=[dma((3,))],
            compiler_params=pltpu.CompilerParams(vmem_limit_bytes=1 << 20),
        )(*outs)

    placed = (
        P(("col", "row"), None),
        P(),
        P(("row", "col"), None),
        P("row", "col", None),
        P("row", "col"),
        P("row", "col"),
    )
    return jax.shard_map(
        body,
        mesh=mesh,
        in_specs=placed,
        out_specs=(P(("row", "col"), None), P(("col", "row"), None), P()),
        check_vma=False,
    )
```

```python
import functools

import jax
import jax.numpy as jnp
from jax import lax
from jax.experimental import pallas as pl
from jax.experimental.pallas import tpu as pltpu
from jax.sharding import PartitionSpec as P

MESH = pl.DeviceIdType.MESH
F32 = jnp.float32
BF16 = jnp.bfloat16
OWN, MATE, NEAR, FAR = 0, 1, 2, 3
PARTS = 8
TAIL = 4
ORDER = (
    (0, 2), (0, 3), (0, 1), (1, 3), (3, 2), (4, 3), (5, 3), (3, 3),
    (7, 3), (6, 2), (1, 2), (4, 2), (3, 1), (2, 2), (4, 1), (2, 3),
    (7, 2), (6, 3), (0, 0), (3, 0), (5, 2), (1, 1), (6, 1), (7, 1),
    (5, 1), (2, 1), (2, 0), (1, 0), (4, 0), (7, 0), (6, 0), (5, 0),
)
RIM = (
    ("P", 2, 0), ("P", 3, 0), ("M", 0, 2), ("P", 1, 0), ("M", 0, 3), ("P", 0, 0),
    ("M", 0, 1), ("M", 1, 3), ("M", 3, 2), ("M", 4, 3), ("M", 5, 3), ("M", 3, 3),
    ("M", 7, 3), ("M", 6, 2), ("M", 1, 2), ("M", 4, 2), ("M", 3, 1), ("M", 2, 2),
    ("M", 4, 1), ("M", 2, 3), ("M", 7, 2), ("M", 6, 3), ("E", 0, 0), ("M", 5, 2),
    ("M", 1, 1), ("M", 6, 1), ("M", 7, 1), ("E", 3, 0), ("M", 5, 1), ("M", 2, 1),
    ("O", 0, 1), ("O", 3, 1), ("E", 1, 0), ("E", 4, 0), ("E", 7, 0), ("E", 5, 0),
    ("O", 0, 2), ("E", 2, 0), ("O", 3, 2), ("E", 6, 0), ("W", 0, 0), ("O", 4, 1),
    ("B", 0, 0), ("O", 1, 1), ("O", 0, 3), ("O", 6, 1), ("O", 7, 1), ("O", 3, 3),
    ("O", 2, 1), ("O", 5, 1), ("B", 1, 0), ("O", 4, 2), ("W", 1, 0), ("O", 1, 2),
    ("O", 6, 2), ("O", 1, 3), ("O", 7, 2), ("O", 4, 3), ("O", 2, 2), ("O", 7, 3),
    ("O", 5, 2), ("B", 2, 0), ("O", 5, 3), ("O", 2, 3), ("O", 6, 3), ("B", 3, 0),
    ("B", 0, 1), ("B", 1, 1), ("W", 2, 0), ("B", 2, 1), ("B", 3, 1),
)
CENTRAL = (
    ("P", 2, 0), ("P", 3, 0), ("P", 1, 0), ("P", 0, 0), ("M", 0, 1), ("J", 0, 2),
    ("J", 0, 3), ("J", 1, 3), ("J", 3, 2), ("M", 3, 1), ("J", 4, 3), ("J", 5, 3),
    ("M", 4, 1), ("J", 3, 3), ("J", 7, 3), ("J", 6, 2), ("J", 1, 2), ("E", 0, 0),
    ("J", 4, 2), ("E", 3, 0), ("J", 2, 2), ("M", 1, 1), ("M", 6, 1), ("J", 2, 3),
    ("M", 7, 1), ("J", 7, 2), ("M", 5, 1), ("J", 6, 3), ("M", 2, 1), ("O", 0, 2),
    ("O", 0, 1), ("J", 5, 2), ("O", 3, 2), ("E", 4, 0), ("E", 1, 0), ("O", 0, 3),
    ("E", 6, 0), ("E", 7, 0), ("O", 3, 1), ("O", 3, 3), ("E", 2, 0), ("E", 5, 0),
    ("W", 0, 0), ("O", 4, 2), ("B", 0, 0), ("O", 1, 1), ("O", 1, 2), ("O", 6, 2),
    ("O", 4, 1), ("O", 1, 3), ("O", 7, 2), ("O", 7, 1), ("O", 4, 3), ("O", 2, 2),
    ("O", 5, 1), ("O", 7, 3), ("O", 5, 2), ("B", 2, 0), ("O", 2, 1), ("W", 1, 0),
    ("O", 5, 3), ("O", 2, 3), ("O", 6, 1), ("B", 1, 0), ("O", 6, 3), ("B", 3, 0),
    ("B", 0, 1), ("B", 2, 1), ("W", 2, 0), ("B", 1, 1), ("B", 3, 1),
)


def split_axis(size, inner):
    while size % inner:
        inner -= 1
    return size // inner, inner


def kernel(
    dims,
    count_ref,
    pos_ref,
    feat_ref,
    weight_ref,
    gout_ref,
    adj_ref,
    act_ref,
    gin_ref,
    gw_ref,
    pos_v,
    inv_v,
    inv_s,
    vals,
    dense,
    dense_t,
    feats,
    pair,
    mine,
    s_in,
    r_in,
    s_out,
    r_out,
    af,
    ghs,
    acc,
    rs_y,
    rr_y,
    rs_z,
    rr_z,
    ws1,
    wr1,
    ws2,
    wr2,
    w4,
    local_sem,
    sem_up,
    sem_sent,
    sem_fx,
    sem_fs,
    sem_c,
    sem_a,
    sem_b,
    sem_ry,
    sem_r0,
    sem_rz,
    sem_w,
):
    (nrow, ncol, ro, ri, co, ci, parts) = dims
    slots, bs, _ = adj_ref.shape
    own, width = feat_ref.shape
    piece = own // parts
    row_blocks = dense.shape[0] // bs
    col_blocks = dense.shape[1] // bs
    spots = row_blocks * col_blocks
    row = lax.axis_index("row")
    col = lax.axis_index("col")
    rx, rc = lax.div(row, ri), lax.rem(row, ri)
    cz, cy = lax.div(col, ci), lax.rem(col, ci)

    def remote(src, dst, send, recv, axis, peer):
        return pltpu.make_async_remote_copy(
            src_ref=src,
            dst_ref=dst,
            send_sem=send,
            recv_sem=recv,
            device_id={axis: peer},
            device_id_type=MESH,
        )

    loads = [
        pltpu.make_async_copy(feat_ref, feats.at[row], local_sem.at[0]),
        pltpu.make_async_copy(pos_ref, pos_v, local_sem.at[3]),
        pltpu.make_async_copy(adj_ref, vals.at[pl.ds(0, slots)], local_sem.at[1]),
        pltpu.make_async_copy(weight_ref, pair.at[0], local_sem.at[2]),
        pltpu.make_async_copy(gout_ref, pair.at[1], local_sem.at[2]),
    ]
    for load in loads[:2]:
        load.start()

    barrier = pltpu.get_barrier_semaphore()
    for d in range(1, nrow):
        pl.semaphore_signal(
            barrier, inc=1, device_id={"row": lax.rem(row + d, nrow)}, device_id_type=MESH
        )
    for e in range(1, ci):
        pl.semaphore_signal(
            barrier, inc=1, device_id={"col": cz * ci + lax.rem(cy + e, ci)}, device_id_type=MESH
        )

    def greet(sem, d):
        at = cz + d

        @pl.when((at >= 0) & (at < co))
        def _():
            for e in range(ci):
                pl.semaphore_signal(
                    sem, inc=1, device_id={"col": at * ci + e}, device_id_type=MESH
                )

    for d in range(1, co):
        greet(barrier, d)
    vals[slots] = jnp.zeros((bs, bs), vals.dtype)
    loads[1].wait()
    slot = lax.broadcasted_iota(jnp.int32, (spots, slots), 1)
    spot = lax.broadcasted_iota(jnp.int32, (spots, slots), 0)
    hit = (pos_v[...] == spot) & (slot < count_ref[0, 0])
    found = slots + jnp.sum(jnp.where(hit, slot - slots, 0), axis=1, keepdims=True)
    inv_v[...] = jnp.broadcast_to(found, (spots, 128)).T[:8]
    table = pltpu.make_async_copy(inv_v, inv_s, local_sem.at[4])
    table.start()
    loads[0].wait()
    for load in loads[2:]:
        load.start()
    pl.semaphore_wait(barrier, nrow - 1 + ci - 1 + cz * ci)
    for d in range(1, co):
        greet(sem_up, -d)

    halves = 2
    half = own // halves

    def feature(block, h, sem, peer):
        at = feats.at[block, pl.ds(h * half, half)]
        return remote(at, at, sem_sent.at[0], sem, "row", peer)

    def feature_x(block, h, d):
        sem = sem_fx.at[(ro - d - 1) * halves + h]
        return feature(block, h, sem, lax.rem(rx + d, ro) * ri + rc)

    def feature_in(block, h):
        for e in range(1, ri):
            feature(block, h, sem_fs.at[0], rx * ri + lax.rem(rc + e, ri)).start()

    for h in range(halves):
        for d in range(1, ro):
            feature_x(row, h, d).start()
    for h in range(halves):
        feature_in(row, h)
    table.wait()
    loads[2].wait()

    def fill(r, carry):
        for c in range(col_blocks):
            tile = vals[inv_s[0, r * col_blocks + c]]
            at = pl.ds(pl.multiple_of(r * bs, bs), bs)
            dense[at, c * bs : (c + 1) * bs] = tile
            dense_t[c * bs : (c + 1) * bs, at] = tile.T
        return carry

    lax.fori_loop(0, row_blocks, fill, 0)
    for h in range(halves):
        for d in range(1, ro):
            block = lax.rem(rx + d, ro) * ri + rc
            feature_x(block, h, ro - d).wait_recv()
            feature_in(block, h)
    if ri > 1:
        at = feats.at[pl.ds(0, ro * (ri - 1))]
        remote(at, at, sem_sent.at[0], sem_fs.at[0], "row", 0).wait_recv()

    def rows(block, size=own):
        return pl.ds(pl.multiple_of(block * size, size), size)

    def forward(block):
        return jnp.dot(
            dense[rows(block), :],
            feats[...].reshape(nrow * own, width),
            preferred_element_type=F32,
        )

    central = lax.rem(lax.div(cz + 1, 2), 2) == 1
    mate = cz + 1 - 2 * lax.rem(cz, 2)
    near = 2 - lax.div(cz, 2)
    place = (cz, mate, near, 3 * (near - 1))

    def cut(q):
        return pl.ds(q * piece, piece)

    def pieces(n, sem):
        at = r_out.at[pl.ds(0, n)]
        remote(at, at, sem_sent.at[0], sem, "col", 0).wait_recv()

    def inner_copy(q, d, e):
        at = d * (ci - 1) + e - 1
        return remote(
            s_in.at[at, cut(q)],
            r_in.at[at, cut(q)],
            sem_sent.at[0],
            sem_c.at[q * 4 + d],
            "col",
            cz * ci + lax.rem(cy + e, ci),
        )

    def partial(targets, queue):
        done = []
        queue = list(queue)
        for d in targets:
            for e in range(1, ci):
                block = place[d] * ci + lax.rem(cy + e, ci)
                s_in[d * (ci - 1) + e - 1] = forward(block).astype(BF16)
            done.append(d)
            while queue and (queue[0][1] in done or d == targets[-1]):
                for e in range(1, ci):
                    inner_copy(*queue[0], e).start()
                queue.pop(0)

    partial((NEAR, FAR, MATE, OWN), ORDER)

    def own_part(d):
        mine[d] = forward(place[d] * ci + cy)

    pltpu.make_async_copy(pair, pair, local_sem.at[2]).wait()

    def joined(q, d, others=()):
        n = ci - 1 + len(others)
        if n:
            pieces(n, sem_c.at[q * 4 + d])
        value = mine[d, cut(q)]
        for e in range(1, ci):
            value = value + r_in[d * (ci - 1) + e - 1, cut(q)].astype(F32)
        for landing in others:
            value = value + r_out[q * 4 + landing].astype(F32)
        return value

    def hop(q, d, landing, peer):
        return remote(
            s_out.at[q * 4 + d],
            r_out.at[q * 4 + landing],
            sem_sent.at[0],
            sem_c.at[q * 4 + (landing if landing > 1 else OWN)],
            "col",
            peer * ci + cy,
        )

    def push(block, q, sem, peer):
        at = ghs.at[block, cut(q)]
        return remote(at, at, sem_sent.at[0], sem, "col", peer)

    def inward(block, q, d):
        for e in range(1, ci):
            sem = sem_b.at[d * (ci - 1) + ci - e - 1]
            push(block, q, sem, cz * ci + lax.rem(cy + e, ci)).start()

    def middle(q, d):
        s_out[q * 4 + d] = joined(q, d).astype(BF16)
        hop(q, d, 0 if d == MATE else d, mate).start()

    def join(q, d):
        s_out[q * 4 + d] = joined(q, d, (d,)).astype(BF16)
        hop(q, d, 1, place[d]).start()

    def end(q, role):
        part = joined(q, OWN, (0, 1)).astype(BF16)
        af[cut(q), :] = part
        hidden = jnp.dot(part, pair[0], preferred_element_type=F32)
        sigma = jax.nn.sigmoid(hidden)
        ghs[col, cut(q)] = (
            pair[1, cut(q)].astype(F32) * sigma * (1.0 + hidden * (1.0 - sigma))
        ).astype(BF16)
        label = NEAR if role == "cen" else FAR
        push(col, q, sem_a.at[q * 3 + label - 1], near * ci + cy).start()
        push(col, q, sem_a.at[q * 3 + MATE - 1], mate * ci + cy).start()
        inward(col, q, OWN)
        act_ref[cut(q), :] = (hidden * sigma).astype(BF16)

    def outer(q, d, role):
        block = place[d] * ci + cy
        push(block, q, sem_a.at[q * 3 + d - 1], 0).wait_recv()
        if role == "cen" and d > 1:
            push(block, q, sem_a.at[q * 3 + d - 1], mate * ci + cy).start()
        inward(block, q, d)

    final = FAR, ci - 1

    def gathered(d, e):
        block = place[d] * ci + lax.rem(cy + e, ci)
        if e:
            at = ghs.at[block]
            remote(at, at, sem_sent.at[0], sem_b.at[d * (ci - 1) + e - 1], "col", 0).wait_recv()
        return block

    def backward(d, others, seen):
        for e in range(1, ci) if others else (0,):
            if (d, e) == final:
                continue
            block = gathered(d, e)
            term = jnp.dot(dense_t[:, rows(block)], ghs[block], preferred_element_type=F32)
            acc[...] = acc[...] + term if seen else term
            seen.append(1)

    rows1 = width // nrow
    rows2 = rows1 // ncol

    def w_send(k, source, target, axis, peer):
        remote(source, target, sem_w.at[0, k], sem_w.at[1, k], axis, peer).start()

    w_refs = (wr1, wr2, w4.at[0, pl.ds(0, nrow - 1)], w4.at[pl.ds(0, ncol - 1)])

    def w_copy(k):
        return remote(w_refs[k], w_refs[k], sem_w.at[0, k], sem_w.at[1, k], "col", 0)

    def weight_step(k):
        if k == 0:
            grad = jnp.dot(af[...].T, ghs[col], preferred_element_type=F32)
            ws1[...] = grad.astype(BF16).reshape(nrow, rows1, width)
            for d in range(1, nrow):
                peer = lax.rem(row + d, nrow)
                w_send(0, ws1.at[peer], wr1.at[d - 1], "row", peer)
        elif k == 1:
            w_copy(0).wait_recv()
            share = ws1[row].astype(F32)
            for d in range(1, nrow):
                share = share + wr1[d - 1].astype(F32)
            for j in range(ncol):
                ws2[j] = share[j * rows2 : (j + 1) * rows2].astype(BF16)
            for d in range(1, ncol):
                peer = lax.rem(col + d, ncol)
                w_send(1, ws2.at[peer], wr2.at[d - 1], "col", peer)
        elif k == 2:
            w_copy(1).wait_recv()
            share = ws2[col].astype(F32)
            for d in range(1, ncol):
                share = share + wr2[d - 1].astype(F32)
            w4[col, row] = share.astype(BF16)
            for d in range(1, nrow):
                at = w4.at[col, row]
                w_send(2, at, at, "row", lax.rem(row + d, nrow))
        elif k == 3:
            w_copy(2).wait_recv()
            for d in range(1, ncol):
                w_send(3, w4.at[col], w4.at[col], "col", lax.rem(col + d, ncol))
        else:
            w_copy(3).wait_recv()
            for r in range(nrow):
                for k in range(ncol):
                    at = r * rows1 + k * rows2
                    gw_ref[at : at + rows2, :] = w4[k, r].astype(F32)

    def act_on(event, role, seen):
        kind, a, b = event
        if kind == "M":
            middle(a, b)
        elif kind == "J":
            join(a, b)
        elif kind == "E":
            end(a, role)
        elif kind == "O":
            outer(a, b, role)
        elif kind == "B":
            backward(a, b, seen)
        elif kind == "P":
            own_part(a)
        else:
            weight_step(a)

    @pl.when(cz < co - 1)
    def _():
        pl.semaphore_wait(sem_up, (co - 1 - cz) * ci)


    @pl.when(central)
    def _():
        seen = []
        for event in CENTRAL:
            act_on(event, "cen", seen)

    @pl.when(jnp.logical_not(central))
    def _():
        seen = []
        for event in RIM:
            act_on(event, "rim", seen)

    block = gathered(*final)
    last = ghs[block]

    def finished(to, core):
        at = rows(to * ri + core)
        return acc[at, :] + jnp.dot(
            dense_t[at, rows(block)], last, preferred_element_type=F32
        )

    chunk = own // TAIL

    def tail_cut(p):
        return pl.ds(p * chunk, chunk)

    def tail_pieces(n, sem):
        at = rr_y.at[pl.ds(0, n), tail_cut(0)]
        remote(at, at, sem_sent.at[0], sem, "row", 0).wait_recv()

    def sibling(d, e, p):
        at = d * (ri - 1) + e - 1
        return remote(
            rs_y.at[at, tail_cut(p)],
            rr_y.at[at, tail_cut(p)],
            sem_sent.at[0],
            sem_ry.at[(d - 1) * TAIL + p] if d else sem_r0.at[0],
            "row",
            rx * ri + lax.rem(rc + e, ri),
        )

    def across(d, p):
        return remote(
            rs_z.at[d - 1, tail_cut(p)],
            rr_z.at[d - 1, tail_cut(p)],
            sem_sent.at[0],
            sem_rz.at[(d - 1) * TAIL + p],
            "row",
            lax.rem(rx + d, ro) * ri + rc,
        )

    def to_siblings(d):
        to = lax.rem(rx + d, ro)
        for e in range(1, ri):
            rs_y[d * (ri - 1) + e - 1] = finished(to, lax.rem(rc + e, ri)).astype(BF16)
            for p in range(TAIL):
                sibling(d, e, p).start()

    def kept(d):
        at = rows(lax.rem(rx + d, ro) * ri + rc)
        acc[at, :] = finished(lax.rem(rx + d, ro), rc)

    for d in range(1, ro):
        to_siblings(d)
    for d in range(1, ro):
        kept(d)
    to_siblings(0)

    def chip_sum(d, p):
        at = pl.ds(pl.multiple_of((lax.rem(rx + d, ro) * ri + rc) * own + p * chunk, chunk), chunk)
        value = acc[at, :]
        for e in range(1, ri):
            value = value + rr_y[d * (ri - 1) + e - 1, tail_cut(p)].astype(F32)
        return value

    for p in range(TAIL):
        for d in range(1, ro):
            if ri > 1:
                tail_pieces(ri - 1, sem_ry.at[(d - 1) * TAIL + p])
            rs_z[d - 1, tail_cut(p)] = chip_sum(d, p).astype(BF16)
            across(d, p).start()
    kept(0)
    weight_step(3)
    if ri > 1:
        at = rr_y.at[pl.ds(0, ri - 1)]
        remote(at, at, sem_sent.at[0], sem_r0.at[0], "row", 0).wait_recv()
    for p in range(TAIL):
        value = chip_sum(0, p)
        for d in range(1, ro):
            across(d, p).wait_recv()
            value = value + rr_z[d - 1, tail_cut(p)].astype(F32)
        gin_ref[tail_cut(p), :] = lax.dot_general(
            value.astype(BF16), pair[0], (((1,), (1,)), ((), ())), preferred_element_type=F32
        ).astype(BF16)
    weight_step(4)

    def all_sent(extra):
        blocks = (ro - 1) + ro * (ri - 1)
        blocks += co * (ci - 1) + (co - 1) + 2 + co * (ci - 1) + extra
        blocks += ro * (ri - 1) + (ro - 1)
        at = dense.at[pl.ds(0, blocks * own * width // dense.shape[1])]
        remote(at, at, sem_sent.at[0], sem_sent.at[0], "row", 0).wait_send()

    @pl.when(central)
    def _():
        all_sent(2)

    @pl.when(jnp.logical_not(central))
    def _():
        all_sent(0)

    for k in range(4):
        w_copy(k).wait_send()


def hand_on(a_in, b_in, c_in, a_out, b_out, c_out, sems):
    copies = [
        pltpu.make_async_copy(source, target, sems.at[k])
        for k, (source, target) in enumerate(((a_in, a_out), (b_in, b_out), (c_in, c_out)))
    ]
    for copy in copies:
        copy.start()
    for copy in copies:
        copy.wait()


def solution(mesh):
    nrow, ncol = mesh.shape["row"], mesh.shape["col"]
    ro, ri = split_axis(nrow, 2)
    co = 4
    ci = ncol // co
    parts = PARTS
    dims = (nrow, ncol, ro, ri, co, ci, parts)

    def body(features, weight, grad_out, adj_values, block_pos, block_count):
        own, width = features.shape
        slots, bs, _ = adj_values.shape
        rows_tile = own * ncol
        cols_tile = own * nrow
        spots = (rows_tile // bs) * (cols_tile // bs)
        piece = own // parts
        rows1 = width // nrow
        rows2 = rows1 // ncol
        dma = pltpu.SemaphoreType.DMA

        def block(n, rows, dtype=BF16):
            return pltpu.VMEM((max(n, 1), rows, width), dtype)

        scratch = [
            pltpu.VMEM((1, slots), jnp.int32),
            pltpu.VMEM((8, spots), jnp.int32),
            pltpu.SMEM((8, spots), jnp.int32),
            pltpu.VMEM((slots + 1, bs, bs), BF16),
            pltpu.VMEM((rows_tile, cols_tile), BF16),
            pltpu.VMEM((cols_tile, rows_tile), BF16),
            block(nrow, own),
            block(2, own),
            block(co, own, F32),
            block(co * (ci - 1), own),
            block(co * (ci - 1), own),
            block(parts * 4, piece),
            block(parts * 4, piece),
            pltpu.VMEM((own, width), BF16),
            block(ncol, own),
            pltpu.VMEM((cols_tile, width), F32),
            block(ro * (ri - 1), own),
            block(ro * (ri - 1), own),
            block(ro - 1, own),
            block(ro - 1, own),
            block(nrow, rows1),
            block(nrow - 1, rows1),
            block(ncol, rows2),
            block(ncol - 1, rows2),
            pltpu.VMEM((ncol, nrow, rows2, width), BF16),
            dma((5,)),
            pltpu.SemaphoreType.REGULAR,
            dma((1,)),
            dma((max(2 * (ro - 1), 1),)),
            dma((1,)),
            dma((parts * 4,)),
            dma((parts * 3,)),
            dma((max(co * (ci - 1), 1),)),
            dma((max(TAIL * (ro - 1), 1),)),
            dma((1,)),
            dma((max(TAIL * (ro - 1), 1),)),
            dma((2, 4)),
        ]
        vmem = pl.BlockSpec(memory_space=pltpu.VMEM)
        anyspace = pl.BlockSpec(memory_space=pl.ANY)
        shapes = (
            jax.ShapeDtypeStruct((own, width), BF16),
            jax.ShapeDtypeStruct((own, width), BF16),
            jax.ShapeDtypeStruct((width, width), F32),
        )
        held = sum(
            2 * ref.dtype.itemsize * functools.reduce(lambda a, b: a * b, ref.shape, 1) // 2
            for ref in scratch
            if getattr(ref, "memory_space", None) == pltpu.VMEM
        )
        outs = pl.pallas_call(
            functools.partial(kernel, dims),
            out_shape=shapes,
            in_specs=[pl.BlockSpec(memory_space=pltpu.SMEM)] + [anyspace] * 5,
            out_specs=[vmem] * 3,
            scratch_shapes=scratch,
            compiler_params=pltpu.CompilerParams(
                collective_id=0,
                has_side_effects=True,
                vmem_limit_bytes=min(held + (6 << 20), 66 * 1000 * 1000),
            ),
        )(
            block_count,
            *(
                pltpu.with_memory_space_constraint(x, pltpu.HBM)
                for x in (block_pos, features, weight, grad_out, adj_values)
            ),
        )
        return pl.pallas_call(
            hand_on,
            out_shape=shapes,
            in_specs=[anyspace] * 3,
            out_specs=[anyspace] * 3,
            scratch_shapes=[dma((3,))],
            compiler_params=pltpu.CompilerParams(vmem_limit_bytes=1 << 20),
        )(*outs)

    placed = (
        P(("col", "row"), None),
        P(),
        P(("row", "col"), None),
        P("row", "col", None),
        P("row", "col"),
        P("row", "col"),
    )
    return jax.shard_map(
        body,
        mesh=mesh,
        in_specs=placed,
        out_specs=(P(("row", "col"), None), P(("col", "row"), None), P()),
        check_vma=False,
    )
```
